32 devices in a mesh: bx: 4 (over y, x), by: 8 (over z, core).
Axes of the slice: x: 2, y: 2, z: 4, core: 2. Of those that a mesh axis runs over, the one named last changes fastest.
Arguments:
- terminal_value: float32 [64, 128, 256], P('bx', 'by'), may hold values from -3 to 3
- density: float32 [64, 128, 256], P('bx', 'by')
- potential: float32 [64, 128, 256], P('bx', 'by'), may hold values from -5 to 5
- heights: int32 [64, 128], P('bx', 'by'), may hold values from 0 to 64
Outputs:
- value_field: float32 [64, 128, 256], P('bx', 'by')
- density_next: float32 [64, 128, 256], P('bx', 'by')
The draws below stay inside these ranges and needn't reach their ends.
All inputs are finite; a program needn't handle non-finite values.
Results may differ from the reference program's by a relative error of at most 0.0001.
Values sent between devices are 32-bit elements; how exact they have to be, the bound alone decides.
A program may use at most 64 MiB of HBM per device.

```python
import jax
import jax.numpy as jnp
from jax import lax

NZ = 256
ITERS = 3
NX = 64
NY = 128


def draw_density(key, part):
    shape = (NX, NY, NZ)
    first = lax.broadcasted_iota(jnp.float32, shape, 0) / NX
    second = lax.broadcasted_iota(jnp.float32, shape, 1) / NY
    ramp = (1.0 + 2.0 * first) * (1.0 + 2.0 * second) / 4.0
    rough = jax.random.uniform(key, shape, jnp.float32, 0.25, 1.75)
    return (ramp * rough).astype(jnp.float32)


def touch_ends(values, rng, least, largest):
    longest = values.shape.index(max(values.shape))
    spots = []
    for shift in (0, 1):
        where = [jax.random.randint(jax.random.fold_in(rng, axis), (), 0, length) for axis, length in enumerate(values.shape)]
        where[longest] = (where[longest] + shift) % values.shape[longest]
        spots.append(tuple(where))
    return values.at[spots[0]].set(least).at[spots[1]].set(largest)


def level_of(stream_key, extent, pieces, smallest, high):
    gain = 1.0
    for dim, shards_of in pieces:
        steps = jax.random.uniform(jax.random.fold_in(jax.random.fold_in(stream_key, 6), dim), (shards_of,), jnp.float32, smallest / len(pieces), high / len(pieces))
        gain = gain * jnp.repeat(jnp.exp(steps), extent[dim] // shards_of).reshape((-1,) + (1,) * (len(extent) - 1 - dim))
    return gain


def scatter_about(own_key, shape, spread, bound, cuts=(), kind=jnp.bfloat16):
    array = jax.random.normal(own_key, shape, jnp.float32) * spread
    if len(cuts) > 0:
        array = level_of(own_key, shape, cuts, -0.22, 0.18) * array
    return jnp.clip(array, min=-bound, max=bound).astype(kind)


def setup_inputs(seed: int = 0) -> dict:
    arg_keys = jax.random.split(jax.random.key(seed), 5)
    terminal_value = scatter_about(arg_keys[0], (NX, NY, NZ), 0.5, 3.0, ((0, 4), (1, 8)), jnp.float32)
    density = draw_density(jax.random.fold_in(arg_keys[4], 71), 0)
    potential = scatter_about(arg_keys[2], (NX, NY, NZ), 1.0, 5.0, ((0, 4), (1, 8)), jnp.float32)
    heights = touch_ends(jax.random.randint(arg_keys[3], (NX, NY), 0, NZ // 4 + 1), jax.random.fold_in(arg_keys[3], 1), 0, (NZ // 4 + 1) - 1).astype(jnp.int32)
    return {"terminal_value": terminal_value, "density": density, "potential": potential, "heights": heights}


DT_HJB = 0.5
NU_HJB = 0.25
COUPLE = 0.5
PENALTY = 2.0
DT_FP = 0.25
DIFFUSE = 1.0
ABSORB = 4.0


def neighbours(padded):
    full = jnp.pad(padded, ((0, 0), (0, 0), (1, 1)))
    centre = full[1:-1, 1:-1, 1:-1]
    pairs = [(full[2:, 1:-1, 1:-1], full[:-2, 1:-1, 1:-1]),
             (full[1:-1, 2:, 1:-1], full[1:-1, :-2, 1:-1]),
             (full[1:-1, 1:-1, 2:], full[1:-1, 1:-1, :-2])]
    return centre, pairs


def hjb_update(padded, cost):
    centre, pairs = neighbours(padded)
    laplace = -6.0 * centre
    hamilton = jnp.zeros_like(centre)
    for upper, lower in pairs:
        laplace = laplace + upper + lower
        hamilton = hamilton + jnp.square(jnp.maximum(centre - lower, 0.0)) + jnp.square(jnp.minimum(upper - centre, 0.0))
    return centre + DT_HJB * (NU_HJB * laplace - 0.5 * hamilton + cost)


def transport(mass_pad, value_pad):
    mass, mass_pairs = neighbours(mass_pad)
    value, value_pairs = neighbours(value_pad)
    divergence = jnp.zeros_like(mass)
    for mass_side, value_side in zip(mass_pairs, value_pairs):
        mass_up, mass_low = mass_side
        value_up, value_low = value_side
        speed_up = value - value_up
        flux_up = jnp.maximum(speed_up, 0.0) * mass + jnp.minimum(speed_up, 0.0) * mass_up
        speed_low = value_low - value
        flux_low = jnp.maximum(speed_low, 0.0) * mass_low + jnp.minimum(speed_low, 0.0) * mass
        divergence = divergence + (flux_up - flux_low)
    return mass - DT_FP * divergence


def operate(padded, diagonal):
    centre, pairs = neighbours(padded)
    total = jnp.zeros_like(centre)
    for upper, lower in pairs:
        total = total + upper + lower
    return diagonal * centre - DIFFUSE * total


def pad_plane(field):
    return jnp.pad(field, ((1, 1), (1, 1), (0, 0)))


def reference(terminal_value, density, potential, heights):
    levels = lax.broadcasted_iota(jnp.int32, (1, 1, NZ), 2)
    blocked = (levels < heights[:, :, None]).astype(jnp.float32)
    cost = potential + COUPLE * density + PENALTY * blocked
    value_mid = hjb_update(pad_plane(terminal_value), cost)
    value_field = hjb_update(pad_plane(value_mid), cost)
    target = transport(pad_plane(density), pad_plane(value_field))
    diagonal = 1.0 + 6.0 * DIFFUSE + ABSORB * blocked
    solution = target
    residual = target - operate(pad_plane(target), diagonal)
    direction = residual
    norm_now = jnp.sum(residual * residual)
    for iteration in range(ITERS):
        image = operate(pad_plane(direction), diagonal)
        alpha = norm_now / jnp.sum(direction * image)
        solution = solution + alpha * direction
        residual = residual - alpha * image
        norm_next = jnp.sum(residual * residual)
        direction = residual + (norm_next / norm_now) * direction
        norm_now = norm_next
    return value_field, solution
```

```python
import functools

import jax
import jax.numpy as jnp
from jax import lax
from jax.experimental import pallas as pl
from jax.experimental.pallas import tpu as pltpu
from jax.sharding import PartitionSpec as P

DT_HJB = 0.5
NU_HJB = 0.25
COUPLE = 0.5
PENALTY = 2.0
DT_FP = 0.25
ABSORB = 4.0
SHIFT = 7.0

X0 = 4
Y0 = 8
MESH = pl.DeviceIdType.MESH


class Link:
    def __init__(self, src, dst, send, recv, device, can_send, can_recv):
        self.copy = pltpu.make_async_remote_copy(
            src_ref=src, dst_ref=dst, send_sem=send, recv_sem=recv,
            device_id=device, device_id_type=MESH)
        self.can_send, self.can_recv = can_send, can_recv

    def start(self):
        pl.when(self.can_send)(lambda: self.copy.start())

    def wait_recv(self):
        pl.when(self.can_recv)(lambda: self.copy.wait_recv())

    def wait_send(self):
        pl.when(self.can_send)(lambda: self.copy.wait_send())


def kernel(nbx, nby, t_in, m_in, p_in, h_in, v_out, s_out,
           T, C, D, M, V, G, B1, Q, D4, POT, HB, PKS, PKR, OUT, PA, PB,
           ssem, rsem, asend, arecv, bsend, brecv, lsem):
    nx, ny, nz = t_in.shape
    bx, by = lax.axis_index("bx"), lax.axis_index("by")
    XE, YE = nx + 2 * X0, ny + 2 * Y0
    X1, Y1 = X0 + nx, Y0 + ny
    barrier = pltpu.get_barrier_semaphore()
    for k in range(1, nby):
        pl.semaphore_signal(barrier, inc=1, device_id=(bx, lax.rem(by + k, nby)), device_id_type=MESH)
    for k in range(1, nbx):
        pl.semaphore_signal(barrier, inc=1, device_id=(lax.rem(bx + k, nbx), by), device_id_type=MESH)

    own = (pl.ds(X0, nx), pl.ds(Y0, ny))
    loads = [
        pltpu.make_async_copy(h_in, HB.at[1, 1], lsem.at[3]),
        pltpu.make_async_copy(m_in, D.at[own], lsem.at[1]),
        pltpu.make_async_copy(p_in, POT, lsem.at[2]),
        pltpu.make_async_copy(t_in, T.at[own], lsem.at[0]),
    ]
    for c in loads:
        c.start()

    has_xl, has_xu = bx > 0, bx < nbx - 1
    has_yl, has_yu = by > 0, by < nby - 1
    count = [0]

    def link(src, dst, device, can_send, can_recv):
        i = count[0]
        count[0] += 1
        return Link(src, dst, ssem.at[i], rsem.at[i], device, can_send, can_recv)

    def to_x_up(src, dst):
        return link(src, dst, (bx + 1, by), has_xu, has_xl)

    def to_x_down(src, dst):
        return link(src, dst, (bx - 1, by), has_xl, has_xu)

    def to_y_up(src, dst):
        return link(src, dst, (bx, by + 1), has_yu, has_yl)

    def to_y_down(src, dst):
        return link(src, dst, (bx, by - 1), has_yl, has_yu)

    def x_links(buf, w):
        rows = pl.ds(Y0, ny)
        return [to_x_up(buf.at[pl.ds(X1 - w, w), rows], buf.at[pl.ds(X0 - w, w), rows]),
                to_x_down(buf.at[pl.ds(X0, w), rows], buf.at[pl.ds(X1, w), rows])]

    def y_links(src, dst, planes):
        return [to_y_up(src.at[0, planes], dst.at[0, planes]),
                to_y_down(src.at[1, planes], dst.at[1, planes])]

    def y_links_field(buf, planes):
        return [to_y_up(buf.at[planes, pl.ds(Y1 - 8, 8)], buf.at[planes, pl.ds(0, 8)]),
                to_y_down(buf.at[planes, pl.ds(Y0, 8)], buf.at[planes, pl.ds(Y1, 8)])]

    def zero_planes(lo):
        for buf in (T, C, D, G):
            buf[pl.ds(lo, X0)] = jnp.zeros((X0, YE, nz), jnp.float32)

    pl.when(jnp.logical_not(has_xl))(lambda: zero_planes(0))
    pl.when(jnp.logical_not(has_xu))(lambda: zero_planes(X1))

    def column(block, x, rows, first):
        line = HB[block[0], block[1], pl.ds(x, 1), :].astype(jnp.float32)
        lanes = lax.broadcasted_iota(jnp.int32, (rows, ny), 1)
        subs = lax.broadcasted_iota(jnp.int32, (rows, ny), 0) + first
        return jnp.sum(jnp.where(lanes == subs, line, 0.0), axis=1, keepdims=True)

    def blocked(block, x, rows, first):
        level = lax.broadcasted_iota(jnp.int32, (rows, nz), 1).astype(jnp.float32)
        return jnp.where(level < column(block, x, rows, first), 1.0, 0.0)

    for c in loads[:3]:
        c.wait()

    @pl.loop(0, nx)
    def _(x):
        b = blocked((1, 1), x, ny, 0)
        D4[X0 + x, pl.ds(Y0, ny), :] = ABSORB * b
        C[X0 + x, pl.ds(Y0, ny), :] = POT[x] + COUPLE * D[X0 + x, pl.ds(Y0, ny), :] + PENALTY * b

    loads[3].wait()
    row8 = lax.broadcasted_iota(jnp.int32, (8, nz), 0)

    def pack(i, with_density):
        ys = pl.ds(Y1 - 8, 8)
        low = pltpu.roll(D[i, ys, :], 3, 0) if with_density else jnp.zeros((8, nz), jnp.float32)
        PKS[0, i] = jnp.where(row8 >= 5, T[i, ys, :], jnp.where(row8 >= 3, pltpu.roll(C[i, ys, :], 5, 0), low))
        ys = pl.ds(Y0, 8)
        high = pltpu.roll(D[i, ys, :], 5, 0) if with_density else jnp.zeros((8, nz), jnp.float32)
        PKS[1, i] = jnp.where(row8 < 3, T[i, ys, :], jnp.where(row8 < 5, pltpu.roll(C[i, ys, :], 3, 0), high))

    @pl.loop(X0, X1)
    def _(i):
        pack(i, True)

    pl.semaphore_wait(barrier, (nby - 1) + (nbx - 1))

    hx = [to_x_up(HB.at[1, 1], HB.at[0, 1]), to_x_down(HB.at[1, 1], HB.at[2, 1])]
    hy = [to_y_up(HB.at[1, 1], HB.at[1, 0]), to_y_down(HB.at[1, 1], HB.at[1, 2])]
    tx, cx, dx = x_links(T, 3), x_links(C, 2), x_links(D, 1)
    py = y_links(PKS, PKR, pl.ds(X0, nx))
    for c in hx + tx + cx + dx + hy + py:
        c.start()
    for c in hx + tx + cx:
        c.wait_recv()
    for i in (X0 - 2, X0 - 1, X1, X1 + 1):
        pack(i, False)
    pc = y_links(PKS, PKR, pl.ds(X0 - 2, 2)) + y_links(PKS, PKR, pl.ds(X1, 2))
    hc = []
    for side, has in ((0, has_xl), (2, has_xu)):
        up, down = has_yu & has, has_yl & has
        rup, rdown = has_yl & has, has_yu & has
        hc.append(link(HB.at[side, 1], HB.at[side, 0], (bx, by + 1), up, rup))
        hc.append(link(HB.at[side, 1], HB.at[side, 2], (bx, by - 1), down, rdown))
    for c in pc + hc:
        c.start()
    for c in dx + hy + py + pc + hc:
        c.wait_recv()

    keep_l = jnp.where(has_yl, 8, 0)
    keep_u = jnp.where(has_yu, 8, 0)

    @pl.loop(X0 - 2, X1 + 2)
    def _(i):
        got = jnp.where(row8 < keep_l, PKR[0, i], 0.0)
        T[i, pl.ds(0, 8), :] = got
        C[i, pl.ds(0, 8), :] = pltpu.roll(got, 3, 0)
        D[i, pl.ds(0, 8), :] = pltpu.roll(got, 5, 0)
        got = jnp.where(row8 < keep_u, PKR[1, i], 0.0)
        T[i, pl.ds(Y1, 8), :] = got
        C[i, pl.ds(Y1, 8), :] = pltpu.roll(got, 5, 0)
        D[i, pl.ds(Y1, 8), :] = pltpu.roll(got, 3, 0)

    rows = lax.broadcasted_iota(jnp.int32, (YE, nz), 0)
    lane = lax.broadcasted_iota(jnp.int32, (YE, nz), 1)
    first_row = jnp.where(has_yl, 0, Y0)
    last_row = jnp.where(has_yu, YE, Y1)
    first_plane = jnp.where(has_xl, 0, X0)
    last_plane = jnp.where(has_xu, XE, X1)

    def inside(i, v):
        end = jnp.where((i >= first_plane) & (i < last_plane), last_row, 0)
        return jnp.where((rows >= first_row) & (rows < end), v, 0.0)

    def sides(v):
        return (pltpu.roll(v, YE - 1, 0), pltpu.roll(v, 1, 0),
                jnp.where(lane == nz - 1, 0.0, pltpu.roll(v, nz - 1, 1)),
                jnp.where(lane == 0, 0.0, pltpu.roll(v, 1, 1)))

    def hjb(src, dst, lo, hi):
        @pl.loop(lo, hi)
        def _(i):
            v = src[i]
            yu, yl, zu, zl = sides(v)
            lap = -6.0 * v
            ham = jnp.zeros_like(v)
            for u, l in ((src[i + 1], src[i - 1]), (yu, yl), (zu, zl)):
                lap = lap + u + l
                ham = ham + jnp.square(jnp.maximum(v - l, 0.0)) + jnp.square(jnp.minimum(u - v, 0.0))
            dst[i] = inside(i, v + DT_HJB * (NU_HJB * lap - 0.5 * ham + C[i]))

    hjb(T, M, X0 - 2, X1 + 2)
    hjb(M, V, X0 - 1, X1 + 1)
    store_v = pltpu.make_async_copy(V.at[own], v_out, lsem.at[0])
    store_v.start()

    mid = slice(Y0, Y1)

    @pl.loop(X0, X1)
    def _(i):
        v, m = V[i], D[i]
        vs, ms = sides(v), sides(m)
        vx = [V[i + 1, pl.ds(Y0, ny), :], V[i - 1, pl.ds(Y0, ny), :]]
        mx = [D[i + 1, pl.ds(Y0, ny), :], D[i - 1, pl.ds(Y0, ny), :]]
        vs = vx + [a[mid] for a in vs]
        ms = mx + [a[mid] for a in ms]
        v, m = v[mid], m[mid]
        div = jnp.zeros_like(m)
        for a in (0, 2, 4):
            s = v - vs[a]
            t = vs[a + 1] - v
            div = div + (jnp.maximum(s, 0.0) * m + jnp.minimum(s, 0.0) * ms[a]
                         - jnp.maximum(t, 0.0) * ms[a + 1] - jnp.minimum(t, 0.0) * m)
        G[i, pl.ds(Y0, ny), :] = m - DT_FP * div

    gx = x_links(G, 4)
    gy = y_links_field(G, pl.ds(X0, nx))
    for c in gx + gy:
        c.start()

    @pl.loop(0, nx)
    def _(x):
        D4[X0 + x, pl.ds(0, 8), :] = ABSORB * blocked((1, 0), x, 8, ny - 8)
        D4[X0 + x, pl.ds(Y1, 8), :] = ABSORB * blocked((1, 2), x, 8, 0)

    def halo_obstacles(side, x, i):
        D4[i, pl.ds(0, 8), :] = ABSORB * blocked((side, 0), x, 8, ny - 8)
        D4[i, pl.ds(Y0, ny), :] = ABSORB * blocked((side, 1), x, ny, 0)
        D4[i, pl.ds(Y1, 8), :] = ABSORB * blocked((side, 2), x, 8, 0)

    @pl.loop(0, 3)
    def _(j):
        halo_obstacles(0, nx - 3 + j, X0 - 3 + j)
        halo_obstacles(2, j, X1 + j)

    for c in gx:
        c.wait_recv()
    gc = y_links_field(G, pl.ds(1, 3)) + y_links_field(G, pl.ds(X1, 3))
    for c in gc:
        c.start()
    for c in gy + gc:
        c.wait_recv()

    def zero_rows(lo):
        G[:, pl.ds(lo, 8), :] = jnp.zeros((XE, 8, nz), jnp.float32)

    pl.when(jnp.logical_not(has_yl))(lambda: zero_rows(0))
    pl.when(jnp.logical_not(has_yu))(lambda: zero_rows(Y1))

    def shifted(src, i):
        v = src[i]
        yu, yl, zu, zl = sides(v)
        return v, D4[i] * v - (src[i + 1] + src[i - 1] + (yu + yl) + (zu + zl))

    R = M

    @pl.loop(X0 - 3, X1 + 3)
    def _(i):
        v, b = shifted(G, i)
        R[i] = inside(i, (1.0 - SHIFT) * v - b)

    @pl.loop(X0 - 2, X1 + 2)
    def _(i):
        B1[i] = inside(i, shifted(R, i)[1])

    @pl.loop(X0 - 1, X1 + 1)
    def _(i):
        Q[i] = inside(i, shifted(B1, i)[1])

    def moments(i, sums):
        ys = pl.ds(Y0, ny)
        r, b = R[i, ys, :], B1[i, ys, :]
        full = Q[i]
        yu = pltpu.roll(full, YE - 1, 0)[mid]
        zu = jnp.where(lane == nz - 1, 0.0, pltpu.roll(full, nz - 1, 1))[mid]
        q = full[mid]
        image = D4[i, ys, :] * q - 2.0 * (Q[i + 1, ys, :] + yu + zu)
        terms = (r * r, r * b, b * b, b * q, q * q, q * image)

        def fold(a):
            a = a.reshape(ny // 8, 8, nz).sum(axis=0)
            return sum(a[:, j:j + 128] for j in range(0, nz, 128))

        return tuple(s + fold(a) for s, a in zip(sums, terms))

    zero = jnp.zeros((8, 128), jnp.float32)
    sums = lax.fori_loop(X0, X1, moments, (zero,) * 6)
    tile_row = lax.broadcasted_iota(jnp.int32, (8, 128), 0)
    tile = zero
    for k, s in enumerate(sums):
        tile = jnp.where(tile_row == k, jnp.sum(s, axis=0, keepdims=True), tile)

    def all_sum(slots, value, n, me, device, send, recv):
        slots[me] = value
        copies = []
        for k in range(1, n):
            c = pltpu.make_async_remote_copy(
                src_ref=slots.at[me], dst_ref=slots.at[me], send_sem=send.at[k - 1], recv_sem=recv.at[k - 1],
                device_id=device(lax.rem(me + k, n)), device_id_type=MESH)
            c.start()
            copies.append(c)
        for k in range(1, n):
            source = lax.rem(me + n - k, n)
            pltpu.make_async_remote_copy(
                src_ref=slots.at[source], dst_ref=slots.at[source], send_sem=send.at[k - 1], recv_sem=recv.at[k - 1],
                device_id=device(source), device_id_type=MESH).wait_recv()
        return copies, jnp.sum(slots[...], axis=0)

    ca, tile = all_sum(PA, tile, nby, by, lambda j: (bx, j), asend, arecv)
    cb, tile = all_sum(PB, tile, nbx, bx, lambda j: (j, by), bsend, brecv)
    tile = jnp.broadcast_to(jnp.sum(tile, axis=1, keepdims=True), (8, 128))
    nu = [tile[k:k + 1] for k in range(6)]

    def dot(p, q, s):
        total = 0.0
        for i, a in enumerate(p):
            for j, b in enumerate(q):
                total = total + a * b * nu[i + j + s]
        return total

    def energy(p):
        return SHIFT * dot(p, p, 0) + dot(p, p, 1)

    def step_of(rr, p):
        return jnp.clip(rr / energy(p), 1.0 / 17.0, 1.0)

    one = jnp.ones_like(nu[0])
    rr = nu[0]
    p, r = (one,), (one,)
    x = None
    for it in range(3):
        a = step_of(rr, p)
        x = [a * c for c in p] if x is None else [x[j] + a * p[j] if j < len(x) else a * p[j] for j in range(len(p))]
        if it == 2:
            break
        image = [SHIFT * c for c in p] + [jnp.zeros_like(one)]
        for j, c in enumerate(p):
            image[j + 1] = image[j + 1] + c
        r = tuple((r[j] if j < len(r) else 0.0) - a * image[j] for j in range(len(image)))
        new = jnp.maximum(dot(r, r, 0), 0.0)
        beta = new / rr
        p = tuple(r[j] + (beta * p[j] if j < len(p) else 0.0) for j in range(len(r)))
        rr = new
    x = [jnp.concatenate([c] * (nz // 128), axis=1) for c in x]

    @pl.loop(X0, X1)
    def _(i):
        ys = pl.ds(Y0, ny)
        OUT[i - X0] = G[i, ys, :] + x[0] * R[i, ys, :] + x[1] * B1[i, ys, :] + x[2] * Q[i, ys, :]

    store_s = pltpu.make_async_copy(OUT, s_out, lsem.at[1])
    store_s.start()
    for c in hx + tx + cx + dx + hy + py + pc + hc + gx + gy + gc:
        c.wait_send()
    for c in ca + cb:
        c.wait_send()
    store_v.wait()
    store_s.wait()


LINKS = 32


def per_device(nbx, nby, t, m, p, h):
    nx, ny, nz = t.shape
    ext = pltpu.VMEM((nx + 2 * X0, ny + 2 * Y0, nz), jnp.float32)
    packed = pltpu.VMEM((2, nx + 2 * X0, 8, nz), jnp.float32)
    block = pltpu.VMEM((nx, ny, nz), jnp.float32)
    any_spec = pl.BlockSpec(memory_space=pl.ANY)
    out = jax.ShapeDtypeStruct(t.shape, jnp.float32)
    return pl.pallas_call(
        functools.partial(kernel, nbx, nby),
        out_shape=(out, out),
        in_specs=[any_spec] * 4,
        out_specs=(any_spec, any_spec),
        scratch_shapes=[ext] * 9 + [
            block, pltpu.VMEM((3, 3, nx, ny), jnp.int32), packed, packed, block,
            pltpu.VMEM((nby, 8, 128), jnp.float32), pltpu.VMEM((nbx, 8, 128), jnp.float32),
            pltpu.SemaphoreType.DMA((LINKS,)), pltpu.SemaphoreType.DMA((LINKS,)),
            pltpu.SemaphoreType.DMA((nby - 1,)), pltpu.SemaphoreType.DMA((nby - 1,)),
            pltpu.SemaphoreType.DMA((nbx - 1,)), pltpu.SemaphoreType.DMA((nbx - 1,)),
            pltpu.SemaphoreType.DMA((4,)),
        ],
        compiler_params=pltpu.CompilerParams(
            collective_id=0, has_side_effects=True, vmem_limit_bytes=32 * 1024 * 1024),
        name="mean_field_step",
    )(t, m, p, h)


def solution(mesh):
    cells, plane = P("bx", "by", None), P("bx", "by")
    return jax.shard_map(
        functools.partial(per_device, mesh.shape["bx"], mesh.shape["by"]),
        mesh=mesh, in_specs=(cells, cells, cells, plane), out_specs=(cells, cells), check_vma=False)
```

```python
import functools

import jax
import jax.numpy as jnp
from jax import lax
from jax.experimental import pallas as pl
from jax.experimental.pallas import tpu as pltpu
from jax.sharding import PartitionSpec as P

DT_HJB = 0.5
NU_HJB = 0.25
COUPLE = 0.5
PENALTY = 2.0
DT_FP = 0.25
ABSORB = 4.0
SHIFT = 7.0

X0 = 4
HALO = 8
MESH = pl.DeviceIdType.MESH


class Link:
    def __init__(self, src, dst, send, recv, device, can_send, can_recv):
        self.copy = pltpu.make_async_remote_copy(
            src_ref=src, dst_ref=dst, send_sem=send, recv_sem=recv,
            device_id=device, device_id_type=MESH)
        self.can_send, self.can_recv = can_send, can_recv

    def start(self):
        pl.when(self.can_send)(lambda: self.copy.start())

    def wait_recv(self):
        pl.when(self.can_recv)(lambda: self.copy.wait_recv())

    def wait_send(self):
        pl.when(self.can_send)(lambda: self.copy.wait_send())


def kernel(nbx, nby, t_in, m_in, p_in, h_in, v_out, s_out,
           T, C, D, M, V, G, B1, Q, D4, POT, HB, PKS, PKR, GR, PA, PB,
           ssem, rsem, asend, arecv, bsend, brecv, lsem):
    nx, ny, nz = POT.shape
    bx, by = lax.axis_index("bx"), lax.axis_index("by")
    XE, YE, X1 = nx + 2 * X0, ny + HALO, X0 + nx
    barrier = pltpu.get_barrier_semaphore()
    for k in range(1, nby):
        pl.semaphore_signal(barrier, inc=1, device_id=(bx, lax.rem(by + k, nby)), device_id_type=MESH)
    for k in range(1, nbx):
        pl.semaphore_signal(barrier, inc=1, device_id=(lax.rem(bx + k, nbx), by), device_id_type=MESH)

    rows = pl.ds(0, ny)
    beyond = pl.ds(ny, HALO)
    loads = [
        pltpu.make_async_copy(h_in, HB.at[1, 1], lsem.at[3]),
        pltpu.make_async_copy(m_in, D.at[pl.ds(X0, nx), rows], lsem.at[1]),
        pltpu.make_async_copy(p_in, POT, lsem.at[2]),
        pltpu.make_async_copy(t_in, T.at[pl.ds(X0, nx), rows], lsem.at[0]),
    ]
    for c in loads:
        c.start()

    has_xl, has_xu = bx > 0, bx < nbx - 1
    has_yl, has_yu = by > 0, by < nby - 1
    count = [0]

    def link(src, dst, device, can_send, can_recv):
        i = count[0]
        count[0] += 1
        return Link(src, dst, ssem.at[i], rsem.at[i], device, can_send, can_recv)

    def x_up(src, dst):
        return link(src, dst, (bx + 1, by), has_xu, has_xl)

    def x_down(src, dst):
        return link(src, dst, (bx - 1, by), has_xl, has_xu)

    def y_up(src, dst, has=True):
        return link(src, dst, (bx, by + 1), has_yu & has, has_yl & has)

    def y_down(src, dst, has=True):
        return link(src, dst, (bx, by - 1), has_yl & has, has_yu & has)

    def x_links(buf, w):
        return [x_up(buf.at[pl.ds(X1 - w, w), rows], buf.at[pl.ds(X0 - w, w), rows]),
                x_down(buf.at[pl.ds(X0, w), rows], buf.at[pl.ds(X1, w), rows])]

    def packed_links(planes):
        return [y_up(PKS.at[0, planes], PKR.at[0, planes]), y_down(PKS.at[1, planes], PKR.at[1, planes])]

    def field_links(planes):
        return [y_up(G.at[planes, pl.ds(ny - 8, 8)], GR.at[0, planes]),
                y_down(G.at[planes, pl.ds(0, 8)], GR.at[1, planes])]

    def zero_planes(lo):
        for buf in (T, C, D, M, V, G, B1, Q):
            buf[pl.ds(lo, X0)] = jnp.zeros((X0, YE, nz), jnp.float32)

    pl.when(jnp.logical_not(has_xl))(lambda: zero_planes(0))
    pl.when(jnp.logical_not(has_xu))(lambda: zero_planes(X1))

    def below(k):
        return jnp.where(has_xl, X0 - k, X0)

    def above(k):
        return jnp.where(has_xu, X1 + k, X1)

    def column(side, part, x, n, first):
        line = HB[side, part, pl.ds(x, 1), :].astype(jnp.float32)
        lanes = lax.broadcasted_iota(jnp.int32, (n, ny), 1)
        subs = lax.broadcasted_iota(jnp.int32, (n, ny), 0) + first
        return jnp.sum(jnp.where(lanes == subs, line, 0.0), axis=1, keepdims=True)

    def level_mask(col, high):
        level = lax.broadcasted_iota(jnp.int32, (col.shape[0], nz), 1).astype(jnp.float32)
        return jnp.where(level < col, high, 0.0)

    for c in loads[:3]:
        c.wait()

    @pl.loop(0, nx)
    def _(x):
        b = level_mask(column(1, 1, x, ny, 0), ABSORB)
        D4[X0 + x, rows, :] = b
        C[X0 + x, rows, :] = POT[x] + COUPLE * D[X0 + x, rows, :] + (PENALTY / ABSORB) * b

    loads[3].wait()
    row8 = lax.broadcasted_iota(jnp.int32, (8, nz), 0)

    def pack(i, with_density):
        ys = pl.ds(ny - 8, 8)
        low = pltpu.roll(D[i, ys, :], 3, 0) if with_density else jnp.zeros((8, nz), jnp.float32)
        PKS[0, i] = jnp.where(row8 >= 5, T[i, ys, :], jnp.where(row8 >= 3, pltpu.roll(C[i, ys, :], 5, 0), low))
        ys = pl.ds(0, 8)
        high = pltpu.roll(D[i, ys, :], 5, 0) if with_density else jnp.zeros((8, nz), jnp.float32)
        PKS[1, i] = jnp.where(row8 < 3, T[i, ys, :], jnp.where(row8 < 5, pltpu.roll(C[i, ys, :], 3, 0), high))

    @pl.loop(X0, X1)
    def _(i):
        pack(i, True)

    pl.semaphore_wait(barrier, (nby - 1) + (nbx - 1))

    hx = [x_up(HB.at[1, 1], HB.at[0, 1]), x_down(HB.at[1, 1], HB.at[2, 1])]
    hy = [y_up(HB.at[1, 1], HB.at[1, 0]), y_down(HB.at[1, 1], HB.at[1, 2])]
    py = packed_links(pl.ds(X0, nx))
    tx, cx, dx = x_links(T, 3), x_links(C, 2), x_links(D, 1)
    for c in hx + hy + tx + py + cx + dx:
        c.start()

    keep = (row8 >= jnp.where(has_yu, 0, 4)) & (row8 < jnp.where(has_yl, 8, 4))
    upper = row8 < 4

    def join(a, b):
        return jnp.where(keep, jnp.where(upper, b, a), 0.0)

    def unpack(i):
        a, b = PKR[0, i], PKR[1, i]
        T[i, beyond, :] = join(a, b)
        C[i, beyond, :] = join(pltpu.roll(a, 3, 0), pltpu.roll(b, 5, 0))
        D[i, beyond, :] = join(pltpu.roll(a, 5, 0), pltpu.roll(b, 3, 0))

    def loop(lo, hi, f):
        @pl.loop(lo, hi)
        def _(i):
            f(i)

    lane = lax.broadcasted_iota(jnp.int32, (YE, 128), 1)

    def z_up(v):
        n = v.shape[0]
        tiles = [pltpu.roll(v[:, j:j + 128], 127, 1) for j in range(0, nz, 128)]
        tiles.append(jnp.zeros_like(tiles[0]))
        return jnp.concatenate([jnp.where(lane[:n] == 127, b, a) for a, b in zip(tiles, tiles[1:])], axis=1)

    def z_low(v, edge=None):
        n = v.shape[0]
        tiles = [jnp.zeros((n, 128), jnp.float32) if edge is None else edge]
        tiles += [pltpu.roll(v[:, j:j + 128], 1, 1) for j in range(0, nz, 128)]
        return jnp.concatenate([jnp.where(lane[:n] == 0, a, b) for a, b in zip(tiles, tiles[1:])], axis=1)

    def put(dst, i, v):
        dst[i, rows, :] = v[:ny]
        dst[i, beyond, :] = jnp.where(keep, v[ny:], 0.0)

    def hjb(src, dst, lo, hi, out=None):
        def f(i):
            v = src[i]
            lap = -6.0 * v
            ham = jnp.zeros_like(v)
            for u, l in ((src[i + 1], src[i - 1]), (pltpu.roll(v, YE - 1, 0), pltpu.roll(v, 1, 0)),
                         (z_up(v), z_low(v))):
                lap = lap + (u + l)
                ham = ham + jnp.square(jnp.maximum(v - l, 0.0)) + jnp.square(jnp.minimum(u - v, 0.0))
            new = v + DT_HJB * (NU_HJB * lap - 0.5 * ham + C[i])
            put(dst, i, new)
            if out is not None:
                out[i - X0] = new[:ny]
        loop(lo, hi, f)

    def flux(v, vu, m, mu):
        s = v - vu
        return jnp.maximum(s, 0.0) * m + jnp.minimum(s, 0.0) * mu

    def x_flux(i):
        return flux(V[i, rows, :], V[i + 1, rows, :], D[i, rows, :], D[i + 1, rows, :])

    def transport(lo, hi):
        def f(i, before):
            v, m = V[i], D[i]
            fy = flux(v, pltpu.roll(v, YE - 1, 0), m, pltpu.roll(m, YE - 1, 0))
            ly = pltpu.roll(fy, 1, 0)[:ny]
            v, m = v[:ny], m[:ny]
            fz = flux(v, z_up(v), m, z_up(m))
            lz = z_low(fz, jnp.minimum(-v[:, :128], 0.0) * m[:, :128])
            fx = x_flux(i)
            G[i, rows, :] = m - DT_FP * ((fx - before) + (fy[:ny] - ly) + (fz - lz))
            return fx
        lax.fori_loop(lo, hi, f, x_flux(lo - 1))

    def beyond_obstacles(side, x, i):
        col = jnp.where(lax.broadcasted_iota(jnp.int32, (8, 1), 0) < 4,
                        column(side, 2, x, 8, 0), column(side, 0, x, 8, ny - 8))
        D4[i, beyond, :] = level_mask(col, ABSORB)

    for c in hy + py:
        c.wait_recv()
    loop(X0, X1, unpack)
    hjb(T, M, X0 + 1, X1 - 1)
    hjb(M, V, X0 + 2, X1 - 2, v_out)
    transport(X0 + 3, X1 - 3)
    loop(0, nx, lambda x: beyond_obstacles(1, x, X0 + x))

    for c in hx + tx + cx:
        c.wait_recv()
    corners = ((0, has_xl, X0 - 2), (2, has_xu, X1))
    pc = []
    for side, has, lo in corners:
        loop(lo, lo + 2, lambda i: pack(i, False))
        pc += packed_links(pl.ds(lo, 2))
        pc.append(y_up(HB.at[side, 1], HB.at[side, 0], has))
        pc.append(y_down(HB.at[side, 1], HB.at[side, 2], has))
    for c in pc:
        c.start()
    for c in dx + pc:
        c.wait_recv()
    for side, has, lo in corners:
        loop(lo, lo + 2, unpack)
    hjb(T, M, below(2), X0 + 1)
    hjb(T, M, X1 - 1, above(2))
    hjb(M, V, below(1), X0)
    hjb(M, V, X1, above(1))
    hjb(M, V, X0, X0 + 2, v_out)
    hjb(M, V, X1 - 2, X1, v_out)
    transport(X0, X0 + 3)
    transport(X1 - 3, X1)

    gx = x_links(G, 4)
    gy = field_links(pl.ds(X0, nx))
    for c in gx + gy:
        c.start()

    def halo_obstacles(side, x, i):
        D4[i, rows, :] = level_mask(column(side, 1, x, ny, 0), ABSORB)
        beyond_obstacles(side, x, i)

    @pl.loop(0, 3)
    def _(j):
        halo_obstacles(0, nx - 3 + j, X0 - 3 + j)
        halo_obstacles(2, j, X1 + j)

    def merge(i):
        G[i, beyond, :] = join(GR[0, i], GR[1, i])

    def shifted(src, i):
        v = src[i]
        return v, D4[i] * v - ((src[i + 1] + src[i - 1]) + (pltpu.roll(v, YE - 1, 0) + pltpu.roll(v, 1, 0))
                               + (z_up(v) + z_low(v)))

    R = M

    def first(lo, hi):
        def f(i):
            v, b = shifted(G, i)
            put(R, i, (1.0 - SHIFT) * v - b)
        loop(lo, hi, f)

    def power(src, dst, lo, hi):
        loop(lo, hi, lambda i: put(dst, i, shifted(src, i)[1]))

    for c in gy:
        c.wait_recv()
    loop(X0, X1, merge)
    first(X0 + 1, X1 - 1)
    power(R, B1, X0 + 2, X1 - 2)
    power(B1, Q, X0 + 3, X1 - 3)

    for c in gx:
        c.wait_recv()
    gc = field_links(pl.ds(1, 3)) + field_links(pl.ds(X1, 3))
    for c in gc:
        c.start()
    for c in gc:
        c.wait_recv()
    loop(1, X0, merge)
    loop(X1, X1 + 3, merge)
    first(below(3), X0 + 1)
    first(X1 - 1, above(3))
    power(R, B1, below(2), X0 + 2)
    power(R, B1, X1 - 2, above(2))
    power(B1, Q, X0, X0 + 3)
    power(B1, Q, X1 - 3, above(1))

    def moments(i, sums):
        r, b = R[i, rows, :], B1[i, rows, :]
        full = Q[i]
        yu = pltpu.roll(full, YE - 1, 0)[:ny]
        q = full[:ny]
        image = D4[i, rows, :] * q - 2.0 * (Q[i + 1, rows, :] + yu + z_up(q))
        terms = (r * r, r * b, b * b, b * q, q * q, q * image)

        def fold(a):
            a = a.reshape(ny // 8, 8, nz).sum(axis=0)
            return sum(a[:, j:j + 128] for j in range(0, nz, 128))

        return tuple(s + fold(a) for s, a in zip(sums, terms))

    zero = jnp.zeros((8, 128), jnp.float32)
    sums = lax.fori_loop(X0, X1, moments, (zero,) * 6)
    tile_row = lax.broadcasted_iota(jnp.int32, (8, 128), 0)
    tile = zero
    for k, s in enumerate(sums):
        tile = jnp.where(tile_row == k, jnp.sum(s, axis=0, keepdims=True), tile)

    def all_sum(slots, value, n, me, device, send, recv):
        slots[me] = value
        copies = []
        for k in range(1, n):
            c = pltpu.make_async_remote_copy(
                src_ref=slots.at[me], dst_ref=slots.at[me], send_sem=send.at[k - 1], recv_sem=recv.at[k - 1],
                device_id=device(lax.rem(me + k, n)), device_id_type=MESH)
            c.start()
            copies.append(c)
        for k in range(1, n):
            source = lax.rem(me + n - k, n)
            pltpu.make_async_remote_copy(
                src_ref=slots.at[source], dst_ref=slots.at[source], send_sem=send.at[k - 1], recv_sem=recv.at[k - 1],
                device_id=device(source), device_id_type=MESH).wait_recv()
        return copies, jnp.sum(slots[...], axis=0)

    ca, tile = all_sum(PA, tile, nby, by, lambda j: (bx, j), asend, arecv)
    cb, tile = all_sum(PB, tile, nbx, bx, lambda j: (j, by), bsend, brecv)
    tile = jnp.broadcast_to(jnp.sum(tile, axis=1, keepdims=True), (8, 128))
    nu = [tile[k:k + 1] for k in range(6)]

    def dot(p, q, s):
        total = 0.0
        for i, a in enumerate(p):
            for j, b in enumerate(q):
                total = total + a * b * nu[i + j + s]
        return total

    def energy(p):
        return SHIFT * dot(p, p, 0) + dot(p, p, 1)

    def step_of(rr, p):
        return jnp.clip(rr / energy(p), 1.0 / 17.0, 1.0)

    one = jnp.ones_like(nu[0])
    rr = nu[0]
    p, r = (one,), (one,)
    x = None
    for it in range(3):
        a = step_of(rr, p)
        x = [a * c for c in p] if x is None else [x[j] + a * p[j] if j < len(x) else a * p[j] for j in range(len(p))]
        if it == 2:
            break
        image = [SHIFT * c for c in p] + [jnp.zeros_like(one)]
        for j, c in enumerate(p):
            image[j + 1] = image[j + 1] + c
        r = tuple((r[j] if j < len(r) else 0.0) - a * image[j] for j in range(len(image)))
        new = jnp.maximum(dot(r, r, 0), 0.0)
        beta = new / rr
        p = tuple(r[j] + (beta * p[j] if j < len(p) else 0.0) for j in range(len(r)))
        rr = new
    x = [jnp.concatenate([c] * (nz // 128), axis=1) for c in x]

    @pl.loop(X0, X1)
    def _(i):
        s_out[i - X0] = G[i, rows, :] + x[0] * R[i, rows, :] + x[1] * B1[i, rows, :] + x[2] * Q[i, rows, :]

    for c in hx + hy + tx + py + cx + dx + pc + gx + gy + gc:
        c.wait_send()
    for c in ca + cb:
        c.wait_send()


LINKS = 32


def per_device(nbx, nby, t, m, p, h):
    nx, ny, nz = t.shape
    ext = pltpu.VMEM((nx + 2 * X0, ny + HALO, nz), jnp.float32)
    packed = pltpu.VMEM((2, nx + 2 * X0, 8, nz), jnp.float32)
    out = jax.ShapeDtypeStruct(t.shape, jnp.float32)
    return pl.pallas_call(
        functools.partial(kernel, nbx, nby),
        out_shape=(out, out),
        in_specs=[pl.BlockSpec(memory_space=pl.ANY)] * 4,
        out_specs=(pl.BlockSpec(memory_space=pltpu.VMEM),) * 2,
        scratch_shapes=[ext] * 9 + [
            pltpu.VMEM((nx, ny, nz), jnp.float32), pltpu.VMEM((3, 3, nx, ny), jnp.int32), packed, packed, packed,
            pltpu.VMEM((nby, 8, 128), jnp.float32), pltpu.VMEM((nbx, 8, 128), jnp.float32),
            pltpu.SemaphoreType.DMA((LINKS,)), pltpu.SemaphoreType.DMA((LINKS,)),
            pltpu.SemaphoreType.DMA((nby - 1,)), pltpu.SemaphoreType.DMA((nby - 1,)),
            pltpu.SemaphoreType.DMA((nbx - 1,)), pltpu.SemaphoreType.DMA((nbx - 1,)),
            pltpu.SemaphoreType.DMA((4,)),
        ],
        compiler_params=pltpu.CompilerParams(collective_id=0, has_side_effects=True),
        name="mean_field_step",
    )(t, m, p, h)


def solution(mesh):
    cells, plane = P("bx", "by", None), P("bx", "by")
    return jax.shard_map(
        functools.partial(per_device, mesh.shape["bx"], mesh.shape["by"]),
        mesh=mesh, in_specs=(cells, cells, cells, plane), out_specs=(cells, cells), check_vma=False)
```

```python
import functools

import jax
import jax.numpy as jnp
from jax import lax
from jax.experimental import pallas as pl
from jax.experimental.pallas import tpu as pltpu
from jax.sharding import PartitionSpec as P

DT_HJB = 0.5
NU_HJB = 0.25
COUPLE = 0.5
PENALTY = 2.0
DT_FP = 0.25
ABSORB = 4.0
SHIFT = 7.0

X0 = 4
HALO = 8
MESH = pl.DeviceIdType.MESH


class Link:
    def __init__(self, src, dst, send, recv, device, can_send, can_recv):
        self.copy = pltpu.make_async_remote_copy(
            src_ref=src, dst_ref=dst, send_sem=send, recv_sem=recv,
            device_id=device, device_id_type=MESH)
        self.can_send, self.can_recv = can_send, can_recv

    def start(self):
        pl.when(self.can_send)(lambda: self.copy.start())

    def wait_recv(self):
        pl.when(self.can_recv)(lambda: self.copy.wait_recv())

    def wait_send(self):
        pl.when(self.can_send)(lambda: self.copy.wait_send())


def kernel(nbx, nby, t_in, m_in, p_in, h_in, v_out, s_out,
           T, C, D, M, V, G, B1, Q, D4, POT, HB, PKS, PKR, GR, PA, PB,
           ssem, rsem, asend, arecv, bsend, brecv, lsem):
    nx, ny, nz = POT.shape
    bx, by = lax.axis_index("bx"), lax.axis_index("by")
    XE, YE, X1 = nx + 2 * X0, ny + HALO, X0 + nx
    barrier = pltpu.get_barrier_semaphore()
    for k in range(1, nby):
        pl.semaphore_signal(barrier, inc=1, device_id=(bx, lax.rem(by + k, nby)), device_id_type=MESH)
    for k in range(1, nbx):
        pl.semaphore_signal(barrier, inc=1, device_id=(lax.rem(bx + k, nbx), by), device_id_type=MESH)

    rows = pl.ds(0, ny)
    beyond = pl.ds(ny, HALO)
    loads = [
        pltpu.make_async_copy(h_in, HB.at[1, 1], lsem.at[3]),
        pltpu.make_async_copy(m_in, D.at[pl.ds(X0, nx), rows], lsem.at[1]),
        pltpu.make_async_copy(p_in, POT, lsem.at[2]),
        pltpu.make_async_copy(t_in, T.at[pl.ds(X0, nx), rows], lsem.at[0]),
    ]
    for c in loads:
        c.start()

    has_xl, has_xu = bx > 0, bx < nbx - 1
    has_yl, has_yu = by > 0, by < nby - 1
    count = [0]

    def link(src, dst, device, can_send, can_recv):
        i = count[0]
        count[0] += 1
        return Link(src, dst, ssem.at[i], rsem.at[i], device, can_send, can_recv)

    def x_up(src, dst):
        return link(src, dst, (bx + 1, by), has_xu, has_xl)

    def x_down(src, dst):
        return link(src, dst, (bx - 1, by), has_xl, has_xu)

    def y_up(src, dst, has=True):
        return link(src, dst, (bx, by + 1), has_yu & has, has_yl & has)

    def y_down(src, dst, has=True):
        return link(src, dst, (bx, by - 1), has_yl & has, has_yu & has)

    def x_links(buf, w):
        return [x_up(buf.at[pl.ds(X1 - w, w), rows], buf.at[pl.ds(X0 - w, w), rows]),
                x_down(buf.at[pl.ds(X0, w), rows], buf.at[pl.ds(X1, w), rows])]

    def packed_links(planes):
        return [y_up(PKS.at[0, planes], PKR.at[0, planes]), y_down(PKS.at[1, planes], PKR.at[1, planes])]

    def field_links(planes):
        return [y_up(G.at[planes, pl.ds(ny - 8, 8)], GR.at[0, planes]),
                y_down(G.at[planes, pl.ds(0, 8)], GR.at[1, planes])]

    def zero_planes(lo):
        for buf in (T, C, D, G):
            buf[pl.ds(lo, X0)] = jnp.zeros((X0, YE, nz), jnp.float32)

    pl.when(jnp.logical_not(has_xl))(lambda: zero_planes(0))
    pl.when(jnp.logical_not(has_xu))(lambda: zero_planes(X1))

    def column(side, part, x, n, first):
        line = HB[side, part, pl.ds(x, 1), :].astype(jnp.float32)
        lanes = lax.broadcasted_iota(jnp.int32, (n, ny), 1)
        subs = lax.broadcasted_iota(jnp.int32, (n, ny), 0) + first
        return jnp.sum(jnp.where(lanes == subs, line, 0.0), axis=1, keepdims=True)

    def level_mask(col, high):
        level = lax.broadcasted_iota(jnp.int32, (col.shape[0], nz), 1).astype(jnp.float32)
        return jnp.where(level < col, high, 0.0)

    for c in loads[:3]:
        c.wait()

    @pl.loop(0, nx)
    def _(x):
        b = level_mask(column(1, 1, x, ny, 0), ABSORB)
        D4[X0 + x, rows, :] = b
        C[X0 + x, rows, :] = POT[x] + COUPLE * D[X0 + x, rows, :] + (PENALTY / ABSORB) * b

    loads[3].wait()
    row8 = lax.broadcasted_iota(jnp.int32, (8, nz), 0)

    def pack(i, with_density):
        ys = pl.ds(ny - 8, 8)
        low = pltpu.roll(D[i, ys, :], 3, 0) if with_density else jnp.zeros((8, nz), jnp.float32)
        PKS[0, i] = jnp.where(row8 >= 5, T[i, ys, :], jnp.where(row8 >= 3, pltpu.roll(C[i, ys, :], 5, 0), low))
        ys = pl.ds(0, 8)
        high = pltpu.roll(D[i, ys, :], 5, 0) if with_density else jnp.zeros((8, nz), jnp.float32)
        PKS[1, i] = jnp.where(row8 < 3, T[i, ys, :], jnp.where(row8 < 5, pltpu.roll(C[i, ys, :], 3, 0), high))

    @pl.loop(X0, X1)
    def _(i):
        pack(i, True)

    pl.semaphore_wait(barrier, (nby - 1) + (nbx - 1))

    hx = [x_up(HB.at[1, 1], HB.at[0, 1]), x_down(HB.at[1, 1], HB.at[2, 1])]
    hy = [y_up(HB.at[1, 1], HB.at[1, 0]), y_down(HB.at[1, 1], HB.at[1, 2])]
    half = nx // 2
    py, pz = packed_links(pl.ds(X0, half)), packed_links(pl.ds(X0 + half, nx - half))
    tx, cx, dx = x_links(T, 3), x_links(C, 2), x_links(D, 1)
    for c in hx + hy + py + tx + pz + cx + dx:
        c.start()

    keep = (row8 >= jnp.where(has_yu, 0, 4)) & (row8 < jnp.where(has_yl, 8, 4))
    upper = row8 < 4

    def join(a, b):
        return jnp.where(keep, jnp.where(upper, b, a), 0.0)

    def unpack(i):
        a, b = PKR[0, i], PKR[1, i]
        T[i, beyond, :] = join(a, b)
        C[i, beyond, :] = join(pltpu.roll(a, 3, 0), pltpu.roll(b, 5, 0))
        D[i, beyond, :] = join(pltpu.roll(a, 5, 0), pltpu.roll(b, 3, 0))

    def loop(lo, hi, f):
        @pl.loop(lo, hi)
        def _(i):
            f(i)

    def pairs(lo, hi, value, store):
        @pl.loop(0, (hi - lo) // 2)
        def _(j):
            i = lo + 2 * j
            a, b = value(i), value(i + 1)
            store(i, a)
            store(i + 1, b)

    def ends(k, e, value, store):
        @pl.loop(0, k + e)
        def _(j):
            i, n = X0 - k + j, X1 - e + j
            a, b = value(i), value(n)
            store(i, a)
            store(n, b)

    def clear(buf, k):
        def zero(lo):
            buf[pl.ds(lo, k)] = jnp.zeros((k, YE, nz), jnp.float32)
        pl.when(jnp.logical_not(has_xl))(lambda: zero(X0 - k))
        pl.when(jnp.logical_not(has_xu))(lambda: zero(X1))

    lane = lax.broadcasted_iota(jnp.int32, (YE, 128), 1)

    def z_up(v):
        n = v.shape[0]
        tiles = [pltpu.roll(v[:, j:j + 128], 127, 1) for j in range(0, nz, 128)]
        tiles.append(jnp.zeros_like(tiles[0]))
        return jnp.concatenate([jnp.where(lane[:n] == 127, b, a) for a, b in zip(tiles, tiles[1:])], axis=1)

    def z_low(v, edge=None):
        n = v.shape[0]
        tiles = [jnp.zeros((n, 128), jnp.float32) if edge is None else edge]
        tiles += [pltpu.roll(v[:, j:j + 128], 1, 1) for j in range(0, nz, 128)]
        return jnp.concatenate([jnp.where(lane[:n] == 0, a, b) for a, b in zip(tiles, tiles[1:])], axis=1)

    def put(dst, i, v):
        dst[i, rows, :] = v[:ny]
        dst[i, beyond, :] = jnp.where(keep, v[ny:], 0.0)

    def hjb(src):
        def f(i):
            v = src[i]
            lap = -6.0 * v
            ham = jnp.zeros_like(v)
            for u, l in ((src[i + 1], src[i - 1]), (pltpu.roll(v, YE - 1, 0), pltpu.roll(v, 1, 0)),
                         (z_up(v), z_low(v))):
                lap = lap + (u + l)
                ham = ham + jnp.square(jnp.maximum(v - l, 0.0)) + jnp.square(jnp.minimum(u - v, 0.0))
            return v + DT_HJB * (NU_HJB * lap - 0.5 * ham + C[i])
        return f

    def put_mid(i, v):
        put(M, i, v)

    def put_halo(i, v):
        put(V, i, v)

    def put_value(i, v):
        put(V, i, v)
        v_out[i - X0] = v[:ny]

    def flux(v, vu, m, mu):
        s = v - vu
        return jnp.maximum(s, 0.0) * m + jnp.minimum(s, 0.0) * mu

    def x_flux(i):
        return flux(V[i, rows, :], V[i + 1, rows, :], D[i, rows, :], D[i + 1, rows, :])

    def transport(starts, n):
        def one(i, before):
            v, m = V[i], D[i]
            fy = flux(v, pltpu.roll(v, YE - 1, 0), m, pltpu.roll(m, YE - 1, 0))
            ly = pltpu.roll(fy, 1, 0)[:ny]
            v, m = v[:ny], m[:ny]
            fz = flux(v, z_up(v), m, z_up(m))
            lz = z_low(fz, jnp.minimum(-v[:, :128], 0.0) * m[:, :128])
            fx = x_flux(i)
            return fx, m - DT_FP * ((fx - before) + (fy[:ny] - ly) + (fz - lz))

        def f(j, before):
            done = [one(lo + j, b) for lo, b in zip(starts, before)]
            for lo, d in zip(starts, done):
                G[lo + j, rows, :] = d[1]
            return tuple(d[0] for d in done)
        lax.fori_loop(0, n, f, tuple(x_flux(lo - 1) for lo in starts))

    def beyond_obstacles(side, x, i):
        col = jnp.where(lax.broadcasted_iota(jnp.int32, (8, 1), 0) < 4,
                        column(side, 2, x, 8, 0), column(side, 0, x, 8, ny - 8))
        D4[i, beyond, :] = level_mask(col, ABSORB)

    for c in hy + py:
        c.wait_recv()
    loop(X0, X0 + half, unpack)
    pairs(X0 + 1, X0 + half - 1, hjb(T), put_mid)
    for c in pz:
        c.wait_recv()
    loop(X0 + half, X1, unpack)
    pairs(X0 + half - 1, X1 - 1, hjb(T), put_mid)
    pairs(X0 + 2, X1 - 2, hjb(M), put_value)
    transport((X0 + 3, X0 + half), half - 3)
    gi = field_links(pl.ds(X0 + 3, nx - 6))
    for c in gi:
        c.start()
    loop(0, nx, lambda x: beyond_obstacles(1, x, X0 + x))

    for c in hx + tx + cx:
        c.wait_recv()
    corners = ((0, has_xl, X0 - 2), (2, has_xu, X1))
    pc = []
    for side, has, lo in corners:
        loop(lo, lo + 2, lambda i: pack(i, False))
        pc += packed_links(pl.ds(lo, 2))
        pc.append(y_up(HB.at[side, 1], HB.at[side, 0], has))
        pc.append(y_down(HB.at[side, 1], HB.at[side, 2], has))
    for c in pc:
        c.start()
    for c in dx + pc:
        c.wait_recv()
    for side, has, lo in corners:
        loop(lo, lo + 2, unpack)
    ends(2, 1, hjb(T), put_mid)
    clear(M, 2)
    ends(0, 2, hjb(M), put_value)
    for i in (X0 - 1, X1):
        put_halo(i, hjb(M)(i))
    clear(V, 1)
    transport((X0, X1 - 3), 3)

    gx = x_links(G, 4)
    gy = field_links(pl.ds(X0, 3)) + field_links(pl.ds(X1 - 3, 3))
    for c in gx + gy:
        c.start()

    def halo_obstacles(side, x, i):
        D4[i, rows, :] = level_mask(column(side, 1, x, ny, 0), ABSORB)
        beyond_obstacles(side, x, i)

    @pl.loop(0, 3)
    def _(j):
        halo_obstacles(0, nx - 3 + j, X0 - 3 + j)
        halo_obstacles(2, j, X1 + j)

    def merge(i):
        G[i, beyond, :] = join(GR[0, i], GR[1, i])

    def shifted(src):
        def f(i):
            v = src[i]
            return D4[i] * v - ((src[i + 1] + src[i - 1]) + (pltpu.roll(v, YE - 1, 0) + pltpu.roll(v, 1, 0))
                                + (z_up(v) + z_low(v)))
        return f

    R = M

    def residual(i):
        return (1.0 - SHIFT) * G[i] - shifted(G)(i)

    def into(dst):
        return lambda i, v: put(dst, i, v)

    for c in gi + gy:
        c.wait_recv()
    loop(X0, X1, merge)
    pairs(X0 + 1, X1 - 1, residual, into(R))
    pairs(X0 + 2, X1 - 2, shifted(R), into(B1))
    pairs(X0 + 3, X1 - 3, shifted(B1), into(Q))

    for c in gx:
        c.wait_recv()
    gc = field_links(pl.ds(1, 3)) + field_links(pl.ds(X1, 3))
    for c in gc:
        c.start()
    for c in gc:
        c.wait_recv()
    loop(1, X0, merge)
    loop(X1, X1 + 3, merge)
    ends(3, 1, residual, into(R))
    clear(R, 3)
    ends(2, 2, shifted(R), into(B1))
    clear(B1, 2)
    ends(1, 3, shifted(B1), into(Q))
    clear(Q, 1)

    def moments(i, sums):
        r, b = R[i, rows, :], B1[i, rows, :]
        full = Q[i]
        yu = pltpu.roll(full, YE - 1, 0)[:ny]
        q = full[:ny]
        image = D4[i, rows, :] * q - 2.0 * (Q[i + 1, rows, :] + yu + z_up(q))
        terms = (r * r, r * b, b * b, b * q, q * q, q * image)

        def fold(a):
            a = a.reshape(ny // 8, 8, nz).sum(axis=0)
            return sum(a[:, j:j + 128] for j in range(0, nz, 128))

        return tuple(s + fold(a) for s, a in zip(sums, terms))

    zero = jnp.zeros((8, 128), jnp.float32)
    sums = lax.fori_loop(X0, X1, moments, (zero,) * 6)
    tile_row = lax.broadcasted_iota(jnp.int32, (8, 128), 0)
    tile = zero
    for k, s in enumerate(sums):
        tile = jnp.where(tile_row == k, jnp.sum(s, axis=0, keepdims=True), tile)
    tile = jnp.sum(tile, axis=1, keepdims=True)
    tile = jnp.sum(jnp.where(tile_row == lane[:8], tile, 0.0), axis=0, keepdims=True)

    def all_sum(slots, value, n, me, device, send, recv):
        slots[me] = value
        copies = []
        for k in range(1, n):
            c = pltpu.make_async_remote_copy(
                src_ref=slots.at[me], dst_ref=slots.at[me], send_sem=send.at[k - 1], recv_sem=recv.at[k - 1],
                device_id=device(lax.rem(me + k, n)), device_id_type=MESH)
            c.start()
            copies.append(c)
        for k in range(1, n):
            source = lax.rem(me + n - k, n)
            pltpu.make_async_remote_copy(
                src_ref=slots.at[source], dst_ref=slots.at[source], send_sem=send.at[k - 1], recv_sem=recv.at[k - 1],
                device_id=device(source), device_id_type=MESH).wait_recv()
        return copies, jnp.sum(slots[...], axis=0)

    ca, tile = all_sum(PA, tile, nby, by, lambda j: (bx, j), asend, arecv)
    cb, tile = all_sum(PB, tile, nbx, bx, lambda j: (j, by), bsend, brecv)
    nu = [jnp.broadcast_to(tile[:, k:k + 1], (1, 128)) for k in range(6)]

    def dot(p, q, s):
        total = 0.0
        for i, a in enumerate(p):
            for j, b in enumerate(q):
                total = total + a * b * nu[i + j + s]
        return total

    def energy(p):
        return SHIFT * dot(p, p, 0) + dot(p, p, 1)

    def step_of(rr, p):
        return jnp.clip(rr / energy(p), 1.0 / 17.0, 1.0)

    one = jnp.ones_like(nu[0])
    rr = nu[0]
    p, r = (one,), (one,)
    x = None
    for it in range(3):
        a = step_of(rr, p)
        x = [a * c for c in p] if x is None else [x[j] + a * p[j] if j < len(x) else a * p[j] for j in range(len(p))]
        if it == 2:
            break
        image = [SHIFT * c for c in p] + [jnp.zeros_like(one)]
        for j, c in enumerate(p):
            image[j + 1] = image[j + 1] + c
        r = tuple((r[j] if j < len(r) else 0.0) - a * image[j] for j in range(len(image)))
        new = jnp.maximum(dot(r, r, 0), 0.0)
        beta = new / rr
        p = tuple(r[j] + (beta * p[j] if j < len(p) else 0.0) for j in range(len(r)))
        rr = new
    x = [jnp.concatenate([c] * (nz // 128), axis=1) for c in x]

    @pl.loop(X0, X1)
    def _(i):
        s_out[i - X0] = G[i, rows, :] + x[0] * R[i, rows, :] + x[1] * B1[i, rows, :] + x[2] * Q[i, rows, :]

    for c in hx + hy + tx + py + pz + cx + dx + pc + gx + gi + gy + gc:
        c.wait_send()
    for c in ca + cb:
        c.wait_send()


LINKS = 40


def per_device(nbx, nby, t, m, p, h):
    nx, ny, nz = t.shape
    ext = pltpu.VMEM((nx + 2 * X0, ny + HALO, nz), jnp.float32)
    packed = pltpu.VMEM((2, nx + 2 * X0, 8, nz), jnp.float32)
    out = jax.ShapeDtypeStruct(t.shape, jnp.float32)
    return pl.pallas_call(
        functools.partial(kernel, nbx, nby),
        out_shape=(out, out),
        in_specs=[pl.BlockSpec(memory_space=pl.ANY)] * 4,
        out_specs=(pl.BlockSpec(memory_space=pltpu.VMEM),) * 2,
        scratch_shapes=[ext] * 9 + [
            pltpu.VMEM((nx, ny, nz), jnp.float32), pltpu.VMEM((3, 3, nx, ny), jnp.int32), packed, packed, packed,
            pltpu.VMEM((nby, 1, 128), jnp.float32), pltpu.VMEM((nbx, 1, 128), jnp.float32),
            pltpu.SemaphoreType.DMA((LINKS,)), pltpu.SemaphoreType.DMA((LINKS,)),
            pltpu.SemaphoreType.DMA((nby - 1,)), pltpu.SemaphoreType.DMA((nby - 1,)),
            pltpu.SemaphoreType.DMA((nbx - 1,)), pltpu.SemaphoreType.DMA((nbx - 1,)),
            pltpu.SemaphoreType.DMA((4,)),
        ],
        compiler_params=pltpu.CompilerParams(collective_id=0, has_side_effects=True, vmem_limit_bytes=56_000_000),
        name="mean_field_step",
    )(t, m, p, h)


def solution(mesh):
    cells, plane = P("bx", "by", None), P("bx", "by")
    return jax.shard_map(
        functools.partial(per_device, mesh.shape["bx"], mesh.shape["by"]),
        mesh=mesh, in_specs=(cells, cells, cells, plane), out_specs=(cells, cells), check_vma=False)
```

```python
import functools

import jax
import jax.numpy as jnp
from jax import lax
from jax.experimental import pallas as pl
from jax.experimental.pallas import tpu as pltpu
from jax.sharding import PartitionSpec as P

DT_HJB = 0.5
NU_HJB = 0.25
COUPLE = 0.5
PENALTY = 2.0
DT_FP = 0.25
ABSORB = 4.0
SHIFT = 7.0

X0 = 4
HALO = 8
MESH = pl.DeviceIdType.MESH


class Link:
    def __init__(self, src, dst, send, recv, device, can_send, can_recv):
        self.copy = pltpu.make_async_remote_copy(
            src_ref=src, dst_ref=dst, send_sem=send, recv_sem=recv,
            device_id=device, device_id_type=MESH)
        self.can_send, self.can_recv = can_send, can_recv

    def start(self):
        pl.when(self.can_send)(lambda: self.copy.start())

    def wait_recv(self):
        pl.when(self.can_recv)(lambda: self.copy.wait_recv())

    def wait_send(self):
        pl.when(self.can_send)(lambda: self.copy.wait_send())


def kernel(nbx, nby, t_in, m_in, p_in, h_in, v_out, s_out,
           T, C, D, M, V, G, B1, Q, D4, POT, HB, PKS, PKR, GR, PA, PB,
           ssem, rsem, asend, arecv, bsend, brecv, lsem):
    nx, ny, nz = POT.shape
    bx, by = lax.axis_index("bx"), lax.axis_index("by")
    XE, YE, X1 = nx + 2 * X0, ny + HALO, X0 + nx
    barrier = pltpu.get_barrier_semaphore()
    for k in range(1, nby):
        pl.semaphore_signal(barrier, inc=1, device_id=(bx, lax.rem(by + k, nby)), device_id_type=MESH)
    for k in range(1, nbx):
        pl.semaphore_signal(barrier, inc=1, device_id=(lax.rem(bx + k, nbx), by), device_id_type=MESH)

    rows = pl.ds(0, ny)
    beyond = pl.ds(ny, HALO)
    loads = [
        pltpu.make_async_copy(h_in, HB.at[1, 1], lsem.at[3]),
        pltpu.make_async_copy(m_in, D.at[pl.ds(X0, nx), rows], lsem.at[1]),
        pltpu.make_async_copy(p_in, POT, lsem.at[2]),
        pltpu.make_async_copy(t_in, T.at[pl.ds(X0, nx), rows], lsem.at[0]),
    ]
    for c in loads:
        c.start()

    has_xl, has_xu = bx > 0, bx < nbx - 1
    has_yl, has_yu = by > 0, by < nby - 1
    count = [0]

    def link(src, dst, device, can_send, can_recv):
        i = count[0]
        count[0] += 1
        return Link(src, dst, ssem.at[i], rsem.at[i], device, can_send, can_recv)

    def x_up(src, dst):
        return link(src, dst, (bx + 1, by), has_xu, has_xl)

    def x_down(src, dst):
        return link(src, dst, (bx - 1, by), has_xl, has_xu)

    def y_up(src, dst, has=True):
        return link(src, dst, (bx, by + 1), has_yu & has, has_yl & has)

    def y_down(src, dst, has=True):
        return link(src, dst, (bx, by - 1), has_yl & has, has_yu & has)

    def x_links(buf, w):
        return [x_up(buf.at[pl.ds(X1 - w, w), rows], buf.at[pl.ds(X0 - w, w), rows]),
                x_down(buf.at[pl.ds(X0, w), rows], buf.at[pl.ds(X1, w), rows])]

    def packed_links(planes):
        return [y_up(PKS.at[0, planes], PKR.at[0, planes]), y_down(PKS.at[1, planes], PKR.at[1, planes])]

    def field_links(planes):
        return [y_up(G.at[planes, pl.ds(ny - 8, 8)], GR.at[0, planes]),
                y_down(G.at[planes, pl.ds(0, 8)], GR.at[1, planes])]

    def zero_planes(lo):
        for buf in (T, C, D, G):
            buf[pl.ds(lo, X0)] = jnp.zeros((X0, YE, nz), jnp.float32)

    pl.when(jnp.logical_not(has_xl))(lambda: zero_planes(0))
    pl.when(jnp.logical_not(has_xu))(lambda: zero_planes(X1))

    def column(side, part, x, n, first):
        line = HB[side, part, pl.ds(x, 1), :].astype(jnp.float32)
        lanes = lax.broadcasted_iota(jnp.int32, (n, ny), 1)
        subs = lax.broadcasted_iota(jnp.int32, (n, ny), 0) + first
        return jnp.sum(jnp.where(lanes == subs, line, 0.0), axis=1, keepdims=True)

    def level_mask(col, high):
        level = lax.broadcasted_iota(jnp.int32, (col.shape[0], nz), 1).astype(jnp.float32)
        return jnp.where(level < col, high, 0.0)

    for c in loads[:3]:
        c.wait()

    @pl.loop(0, nx)
    def _(x):
        b = level_mask(column(1, 1, x, ny, 0), ABSORB)
        D4[X0 + x, rows, :] = b
        C[X0 + x, rows, :] = POT[x] + COUPLE * D[X0 + x, rows, :] + (PENALTY / ABSORB) * b

    loads[3].wait()
    row8 = lax.broadcasted_iota(jnp.int32, (8, nz), 0)

    def pack(i, with_density):
        ys = pl.ds(ny - 8, 8)
        low = pltpu.roll(D[i, ys, :], 3, 0) if with_density else jnp.zeros((8, nz), jnp.float32)
        PKS[0, i] = jnp.where(row8 >= 5, T[i, ys, :], jnp.where(row8 >= 3, pltpu.roll(C[i, ys, :], 5, 0), low))
        ys = pl.ds(0, 8)
        high = pltpu.roll(D[i, ys, :], 5, 0) if with_density else jnp.zeros((8, nz), jnp.float32)
        PKS[1, i] = jnp.where(row8 < 3, T[i, ys, :], jnp.where(row8 < 5, pltpu.roll(C[i, ys, :], 3, 0), high))

    @pl.loop(X0, X1)
    def _(i):
        pack(i, True)

    pl.semaphore_wait(barrier, (nby - 1) + (nbx - 1))

    hx = [x_up(HB.at[1, 1], HB.at[0, 1]), x_down(HB.at[1, 1], HB.at[2, 1])]
    hy = [y_up(HB.at[1, 1], HB.at[1, 0]), y_down(HB.at[1, 1], HB.at[1, 2])]
    half = nx // 2
    py, pz = packed_links(pl.ds(X0, half)), packed_links(pl.ds(X0 + half, nx - half))
    tx, cx, dx = x_links(T, 3), x_links(C, 2), x_links(D, 1)
    for c in hx + hy + py + tx + pz + cx + dx:
        c.start()

    keep = (row8 >= jnp.where(has_yu, 0, 4)) & (row8 < jnp.where(has_yl, 8, 4))
    upper = row8 < 4

    def join(a, b):
        return jnp.where(keep, jnp.where(upper, b, a), 0.0)

    def unpack(i):
        a, b = PKR[0, i], PKR[1, i]
        T[i, beyond, :] = join(a, b)
        C[i, beyond, :] = join(pltpu.roll(a, 3, 0), pltpu.roll(b, 5, 0))
        D[i, beyond, :] = join(pltpu.roll(a, 5, 0), pltpu.roll(b, 3, 0))

    def loop(lo, hi, f):
        step = 4 if (hi - lo) % 4 == 0 else 1

        @pl.loop(0, (hi - lo) // step)
        def _(j):
            for k in range(step):
                f(lo + step * j + k)

    def pairs(lo, hi, value, store):
        @pl.loop(0, (hi - lo) // 2)
        def _(j):
            i = lo + 2 * j
            a, b = value(i), value(i + 1)
            store(i, a)
            store(i + 1, b)

    def ends(k, e, value, store):
        @pl.loop(0, k + e)
        def _(j):
            i, n = X0 - k + j, X1 - e + j
            a, b = value(i), value(n)
            store(i, a)
            store(n, b)

    def clear(buf, k):
        def zero(lo):
            buf[pl.ds(lo, k)] = jnp.zeros((k, YE, nz), jnp.float32)
        pl.when(jnp.logical_not(has_xl))(lambda: zero(X0 - k))
        pl.when(jnp.logical_not(has_xu))(lambda: zero(X1))

    lane = lax.broadcasted_iota(jnp.int32, (YE, 128), 1)

    def z_up(v):
        n = v.shape[0]
        tiles = [pltpu.roll(v[:, j:j + 128], 127, 1) for j in range(0, nz, 128)]
        tiles.append(jnp.zeros_like(tiles[0]))
        return jnp.concatenate([jnp.where(lane[:n] == 127, b, a) for a, b in zip(tiles, tiles[1:])], axis=1)

    def z_low(v, edge=None):
        n = v.shape[0]
        tiles = [jnp.zeros((n, 128), jnp.float32) if edge is None else edge]
        tiles += [pltpu.roll(v[:, j:j + 128], 1, 1) for j in range(0, nz, 128)]
        return jnp.concatenate([jnp.where(lane[:n] == 0, a, b) for a, b in zip(tiles, tiles[1:])], axis=1)

    def put(dst, i, v):
        dst[i, rows, :] = v[:ny]
        dst[i, beyond, :] = jnp.where(keep, v[ny:], 0.0)

    def hjb(src):
        def f(i):
            v = src[i]
            lap = -6.0 * v
            ham = jnp.zeros_like(v)
            for u, l in ((src[i + 1], src[i - 1]), (pltpu.roll(v, YE - 1, 0), pltpu.roll(v, 1, 0)),
                         (z_up(v), z_low(v))):
                lap = lap + (u + l)
                ham = ham + jnp.square(jnp.maximum(v - l, 0.0)) + jnp.square(jnp.minimum(u - v, 0.0))
            return v + DT_HJB * (NU_HJB * lap - 0.5 * ham + C[i])
        return f

    def put_mid(i, v):
        put(M, i, v)

    def put_halo(i, v):
        put(V, i, v)

    def put_value(i, v):
        put(V, i, v)
        v_out[i - X0] = v[:ny]

    def flux(v, vu, m, mu):
        s = v - vu
        return jnp.maximum(s, 0.0) * m + jnp.minimum(s, 0.0) * mu

    def x_flux(i):
        return flux(V[i, rows, :], V[i + 1, rows, :], D[i, rows, :], D[i + 1, rows, :])

    def transport(starts, n):
        def one(i, before):
            v, m = V[i], D[i]
            fy = flux(v, pltpu.roll(v, YE - 1, 0), m, pltpu.roll(m, YE - 1, 0))
            ly = pltpu.roll(fy, 1, 0)[:ny]
            v, m = v[:ny], m[:ny]
            fz = flux(v, z_up(v), m, z_up(m))
            lz = z_low(fz, jnp.minimum(-v[:, :128], 0.0) * m[:, :128])
            fx = x_flux(i)
            return fx, m - DT_FP * ((fx - before) + (fy[:ny] - ly) + (fz - lz))

        def f(j, before):
            done = [one(lo + j, b) for lo, b in zip(starts, before)]
            for lo, d in zip(starts, done):
                G[lo + j, rows, :] = d[1]
            return tuple(d[0] for d in done)
        lax.fori_loop(0, n, f, tuple(x_flux(lo - 1) for lo in starts))

    def beyond_obstacles(side, x, i):
        col = jnp.where(lax.broadcasted_iota(jnp.int32, (8, 1), 0) < 4,
                        column(side, 2, x, 8, 0), column(side, 0, x, 8, ny - 8))
        D4[i, beyond, :] = level_mask(col, ABSORB)

    for c in hy + py:
        c.wait_recv()
    loop(X0, X0 + half, unpack)
    pairs(X0 + 1, X0 + half - 1, hjb(T), put_mid)
    for c in pz:
        c.wait_recv()
    loop(X0 + half, X1, unpack)
    pairs(X0 + half - 1, X1 - 1, hjb(T), put_mid)
    pairs(X0 + 2, X1 - 2, hjb(M), put_value)
    for c in hx + tx + cx:
        c.wait_recv()
    corners = ((0, has_xl, X0 - 2), (2, has_xu, X1))
    pc = []
    for side, has, lo in corners:
        loop(lo, lo + 2, lambda i: pack(i, False))
        pc += packed_links(pl.ds(lo, 2))
        pc.append(y_up(HB.at[side, 1], HB.at[side, 0], has))
        pc.append(y_down(HB.at[side, 1], HB.at[side, 2], has))
    for c in pc:
        c.start()
    transport((X0 + 3, X0 + half), half - 3)
    gi = field_links(pl.ds(X0 + 3, nx - 6))
    for c in gi:
        c.start()
    loop(0, nx, lambda x: beyond_obstacles(1, x, X0 + x))

    for c in dx + pc:
        c.wait_recv()
    for side, has, lo in corners:
        loop(lo, lo + 2, unpack)
    ends(2, 1, hjb(T), put_mid)
    clear(M, 2)
    ends(0, 2, hjb(M), put_value)
    for i in (X0 - 1, X1):
        put_halo(i, hjb(M)(i))
    clear(V, 1)
    transport((X0, X1 - 3), 3)

    gx = x_links(G, 4)
    gy = field_links(pl.ds(X0, 3)) + field_links(pl.ds(X1 - 3, 3))
    for c in gx + gy:
        c.start()

    def halo_obstacles(side, x, i):
        D4[i, rows, :] = level_mask(column(side, 1, x, ny, 0), ABSORB)
        beyond_obstacles(side, x, i)

    @pl.loop(0, 3)
    def _(j):
        halo_obstacles(0, nx - 3 + j, X0 - 3 + j)
        halo_obstacles(2, j, X1 + j)

    def merge(i):
        G[i, beyond, :] = join(GR[0, i], GR[1, i])

    def shifted(src):
        def f(i):
            v = src[i]
            return D4[i] * v - ((src[i + 1] + src[i - 1]) + (pltpu.roll(v, YE - 1, 0) + pltpu.roll(v, 1, 0))
                                + (z_up(v) + z_low(v)))
        return f

    R = M

    def residual(i):
        return (1.0 - SHIFT) * G[i] - shifted(G)(i)

    def into(dst):
        return lambda i, v: put(dst, i, v)

    def moments(i, sums):
        r, b = R[i, rows, :], B1[i, rows, :]
        full = Q[i]
        yu = pltpu.roll(full, YE - 1, 0)[:ny]
        q = full[:ny]
        image = D4[i, rows, :] * q - 2.0 * (Q[i + 1, rows, :] + yu + z_up(q))
        terms = (r * r, r * b, b * b, b * q, q * q, q * image)

        def fold(a):
            a = a.reshape(ny // 8, 8, nz).sum(axis=0)
            return sum(a[:, j:j + 128] for j in range(0, nz, 128))

        return tuple(s + fold(a) for s, a in zip(sums, terms))

    for c in gi + gy:
        c.wait_recv()
    loop(X0, X1, merge)
    pairs(X0 + 1, X1 - 1, residual, into(R))
    pairs(X0 + 2, X1 - 2, shifted(R), into(B1))
    for c in gx:
        c.wait_recv()
    gc = field_links(pl.ds(1, 3)) + field_links(pl.ds(X1, 3))
    for c in gc:
        c.start()
    pairs(X0 + 3, X1 - 3, shifted(B1), into(Q))

    def two(j, sums):
        return moments(X0 + 4 + 2 * j, moments(X0 + 3 + 2 * j, sums))

    zero = jnp.zeros((8, 128), jnp.float32)
    sums = lax.fori_loop(0, (nx - 8) // 2, two, (zero,) * 6)

    for c in gc:
        c.wait_recv()
    loop(1, X0, merge)
    loop(X1, X1 + 3, merge)
    ends(3, 1, residual, into(R))
    clear(R, 3)
    ends(2, 2, shifted(R), into(B1))
    clear(B1, 2)
    ends(1, 3, shifted(B1), into(Q))
    clear(Q, 1)

    def rest(j, sums):
        for k in (2 * j, 2 * j + 1):
            sums = moments(X0 + k + jnp.where(k >= 3, nx - 8, 0), sums)
        return sums

    sums = lax.fori_loop(0, 4, rest, sums)
    tile_row = lax.broadcasted_iota(jnp.int32, (8, 128), 0)
    tile = zero
    for k, s in enumerate(sums):
        tile = jnp.where(tile_row == k, jnp.sum(s, axis=0, keepdims=True), tile)
    tile = jnp.sum(tile, axis=1, keepdims=True)
    tile = jnp.sum(jnp.where(tile_row == lane[:8], tile, 0.0), axis=0, keepdims=True)

    def all_sum(slots, value, n, me, device, send, recv):
        slots[me] = value
        copies = []
        for k in range(1, n):
            c = pltpu.make_async_remote_copy(
                src_ref=slots.at[me], dst_ref=slots.at[me], send_sem=send.at[k - 1], recv_sem=recv.at[k - 1],
                device_id=device(lax.rem(me + k, n)), device_id_type=MESH)
            c.start()
            copies.append(c)
        for k in range(1, n):
            source = lax.rem(me + n - k, n)
            pltpu.make_async_remote_copy(
                src_ref=slots.at[source], dst_ref=slots.at[source], send_sem=send.at[k - 1], recv_sem=recv.at[k - 1],
                device_id=device(source), device_id_type=MESH).wait_recv()
        return copies, jnp.sum(slots[...], axis=0)

    ca, tile = all_sum(PA, tile, nby, by, lambda j: (bx, j), asend, arecv)
    cb, tile = all_sum(PB, tile, nbx, bx, lambda j: (j, by), bsend, brecv)
    nu = [jnp.broadcast_to(tile[:, k:k + 1], (1, 128)) for k in range(6)]

    def dot(p, q, s):
        total = 0.0
        for i, a in enumerate(p):
            for j, b in enumerate(q):
                total = total + a * b * nu[i + j + s]
        return total

    def energy(p):
        return SHIFT * dot(p, p, 0) + dot(p, p, 1)

    def step_of(rr, p):
        return jnp.clip(rr / energy(p), 1.0 / 17.0, 1.0)

    one = jnp.ones_like(nu[0])
    rr = nu[0]
    p, r = (one,), (one,)
    x = None
    for it in range(3):
        a = step_of(rr, p)
        x = [a * c for c in p] if x is None else [x[j] + a * p[j] if j < len(x) else a * p[j] for j in range(len(p))]
        if it == 2:
            break
        image = [SHIFT * c for c in p] + [jnp.zeros_like(one)]
        for j, c in enumerate(p):
            image[j + 1] = image[j + 1] + c
        r = tuple((r[j] if j < len(r) else 0.0) - a * image[j] for j in range(len(image)))
        new = jnp.maximum(dot(r, r, 0), 0.0)
        beta = new / rr
        p = tuple(r[j] + (beta * p[j] if j < len(p) else 0.0) for j in range(len(r)))
        rr = new
    x = [jnp.concatenate([c] * (nz // 128), axis=1) for c in x]

    def finish(i):
        s_out[i - X0] = G[i, rows, :] + x[0] * R[i, rows, :] + x[1] * B1[i, rows, :] + x[2] * Q[i, rows, :]

    loop(X0, X1, finish)

    for c in hx + hy + tx + py + pz + cx + dx + pc + gx + gi + gy + gc:
        c.wait_send()
    for c in ca + cb:
        c.wait_send()


LINKS = 40


def per_device(nbx, nby, t, m, p, h):
    nx, ny, nz = t.shape
    ext = pltpu.VMEM((nx + 2 * X0, ny + HALO, nz), jnp.float32)
    packed = pltpu.VMEM((2, nx + 2 * X0, 8, nz), jnp.float32)
    out = jax.ShapeDtypeStruct(t.shape, jnp.float32)
    return pl.pallas_call(
        functools.partial(kernel, nbx, nby),
        out_shape=(out, out),
        in_specs=[pl.BlockSpec(memory_space=pl.ANY)] * 4,
        out_specs=(pl.BlockSpec(memory_space=pltpu.VMEM),) * 2,
        scratch_shapes=[ext] * 9 + [
            pltpu.VMEM((nx, ny, nz), jnp.float32), pltpu.VMEM((3, 3, nx, ny), jnp.int32), packed, packed, packed,
            pltpu.VMEM((nby, 1, 128), jnp.float32), pltpu.VMEM((nbx, 1, 128), jnp.float32),
            pltpu.SemaphoreType.DMA((LINKS,)), pltpu.SemaphoreType.DMA((LINKS,)),
            pltpu.SemaphoreType.DMA((nby - 1,)), pltpu.SemaphoreType.DMA((nby - 1,)),
            pltpu.SemaphoreType.DMA((nbx - 1,)), pltpu.SemaphoreType.DMA((nbx - 1,)),
            pltpu.SemaphoreType.DMA((4,)),
        ],
        compiler_params=pltpu.CompilerParams(collective_id=0, has_side_effects=True, vmem_limit_bytes=56_000_000),
        name="mean_field_step",
    )(t, m, p, h)


def solution(mesh):
    cells, plane = P("bx", "by", None), P("bx", "by")
    return jax.shard_map(
        functools.partial(per_device, mesh.shape["bx"], mesh.shape["by"]),
        mesh=mesh, in_specs=(cells, cells, cells, plane), out_specs=(cells, cells), check_vma=False)
```
